32 devices in a mesh: leaf: 32 (over z, y, x, core).
Axes of the slice: x: 2, y: 2, z: 4, core: 2. Of those that a mesh axis runs over, the one named last changes fastest.
Arguments:
- points: bfloat16 [49152, 128], P('leaf'), may hold values from -20 to 20
- weights: bfloat16 [49152, 256], P('leaf'), may hold values from -4 to 4
- targets: bfloat16 [49152, 256], P('leaf'), may hold values from -4 to 4
- near_mask: int32 [32, 4], P('leaf'), may hold values from 0 to 1, as said below
- leaf_skeleton: int32 [32, 256], P('leaf'), may hold values from 0 to 1535, as said below
- node_skeleton: int32 [4, 32, 256], P(None, 'leaf'), may hold values from 0 to 511, as said below
Outputs:
- updated: bfloat16 [49152, 256], P('leaf')
- residual: float32 [49152, 256], P('leaf')
The draws below stay inside these ranges and needn't reach their ends.
Inputs may be any that keep to these rules, and one draw needn't show every extreme that they name: near_mask is 0 where the listed leaf would lie outside the tree; leaf i lists leaf j exactly when leaf j lists leaf i; the number of listed leaves differs from leaf to leaf. `leaf_skeleton`: row i holds 256 distinct increasing point numbers counted within leaf i. `node_skeleton`: entry [l, i] holds 256 distinct increasing positions in the union of the two children's skeletons of the level l + 1 node containing leaf i; equal for all leaves of that node.
All inputs are finite; a program needn't handle non-finite values.
Results may differ from the reference program's by a relative error of at most 0.0034.
Values may be sent and summed in bfloat16 or wider, within the bound.
A program may use at most 64 MiB of HBM per device.

```python
import math
import jax
import jax.numpy as jnp
from jax import lax

F = 128
R = 256
S = 256
PTS_DEV = 1536
LEVELS = 5
REACH = 2
LEAVES = 32
NPTS = 49152


def draw_points(key, part):
    latent_dims = max(F // 16, 4)
    bound = float(F // 8 + 4)
    spread = (0.2 * F) ** 0.5
    radius = (0.75 * F) ** 0.5
    noise_scale = 0.5 ** 0.5
    column = jnp.arange(F, dtype=jnp.int32)[None, :]
    leaf_pos = (jnp.arange(NPTS, dtype=jnp.int32) // PTS_DEV).astype(jnp.float32)[:, None]
    angle = 2.0 * math.pi * leaf_pos / 64.0
    helix = jnp.where(column == latent_dims, radius * jnp.cos(angle), 0.0)
    helix = helix + jnp.where(column == latent_dims + 1, radius * jnp.sin(angle), 0.0)
    key_base = jax.random.fold_in(key, 5)
    base = jnp.clip(jax.random.normal(key_base, (NPTS, F), jnp.float32), -6.0, 6.0)
    latent_scale = spread * jnp.ones((NPTS, 1), jnp.float32)
    scale = jnp.where(column < latent_dims, latent_scale, noise_scale)
    values = jnp.clip(helix + scale * base, -bound, bound)
    return values.astype(jnp.bfloat16)


def draw_near_mask(key, part):
    bits = jax.random.randint(jax.random.fold_in(key, 11), (LEAVES, REACH), 0, 2).astype(jnp.int32)
    leaf_ids = jnp.arange(LEAVES, dtype=jnp.int32)[:, None]
    offsets = jnp.arange(1, REACH + 1, dtype=jnp.int32)[None, :]
    ahead = jnp.where(leaf_ids + offsets < LEAVES, bits, 0)
    source_rows = jnp.clip(leaf_ids - offsets, 0, LEAVES - 1)
    source_cols = jnp.broadcast_to(offsets - 1, (LEAVES, REACH))
    behind = jnp.where(leaf_ids - offsets >= 0, ahead[source_rows, source_cols], 0)
    return jnp.concatenate([ahead, behind], axis=1).astype(jnp.int32)


def draw_leaf_skeleton(key, part):
    keys = jax.random.split(jax.random.fold_in(key, 23), LEAVES)

    def choose(single):
        return jnp.sort(jax.random.permutation(single, PTS_DEV)[:S])
    return jax.vmap(choose)(keys).astype(jnp.int32)


def draw_node_skeleton(key, part):
    base = jax.random.fold_in(key, 37)
    leaf_ids = jnp.arange(LEAVES, dtype=jnp.int32)
    level_ids = jnp.arange(LEVELS - 1, dtype=jnp.int32)

    def per_level(tree_level):

        def per_leaf(index):
            single = jax.random.fold_in(jax.random.fold_in(base, tree_level), jnp.right_shift(index, tree_level + 1))
            return jnp.sort(jax.random.permutation(single, 2 * S)[:S])
        return jax.vmap(per_leaf)(leaf_ids)
    return jax.vmap(per_level)(level_ids).astype(jnp.int32)


def steps_of(key, extent, shards, least, largest):
    loudness, own = 1.0, jax.random.fold_in(key, 6)
    for dim, shards_of in shards:
        draws = jnp.exp(jax.random.uniform(jax.random.fold_in(own, dim), (shards_of,), jnp.float32, least / len(shards), largest / len(shards)))
        loudness = loudness * jnp.repeat(draws, extent[dim] // shards_of).reshape([-1 if axis == dim else 1 for axis in range(len(extent))])
    return loudness


def normal_values(stream_key, dims, scale, reach, shards=(), held_as=jnp.bfloat16):
    drawn = jax.random.normal(stream_key, dims, jnp.float32) * scale
    if len(shards) > 0:
        drawn = steps_of(stream_key, dims, shards, -0.22, 0.18) * drawn
    return jnp.clip(drawn, min=-reach, max=reach).astype(held_as)


def setup_inputs(seed: int = 0) -> dict:
    streams_of = jax.random.split(jax.random.key(seed), 7)
    return {
        "points": draw_points(jax.random.fold_in(streams_of[6], 71), 0),
        "weights": normal_values(streams_of[1], (NPTS, R), 1.0, 4.0, ((0, 32),)),
        "targets": normal_values(streams_of[2], (NPTS, R), 1.0, 4.0, ((0, 32),)),
        "near_mask": draw_near_mask(jax.random.fold_in(streams_of[6], 71), 0),
        "leaf_skeleton": draw_leaf_skeleton(jax.random.fold_in(streams_of[6], 71), 0),
        "node_skeleton": draw_node_skeleton(jax.random.fold_in(streams_of[6], 71), 0),
    }


ridge_weight = 1.0
damping = 0.25


def kernel(left_rows, right_rows):
    left_sq = jnp.sum(jnp.square(left_rows.astype(jnp.float32)), axis=1)
    right_sq = jnp.sum(jnp.square(right_rows.astype(jnp.float32)), axis=1)
    products = lax.dot_general(left_rows, right_rows, (((1,), (1,)), ((), ())), preferred_element_type=jnp.float32)
    return jnp.exp(-(left_sq[:, None] + right_sq[None, :] - 2.0 * products) / left_rows.shape[1])


def apply_tile(own_points, remote_points, remote_weights):
    return jnp.dot(kernel(own_points, remote_points).astype(jnp.bfloat16), remote_weights, preferred_element_type=jnp.float32)


def reference(points, weights, targets, near_mask, leaf_skeleton, node_skeleton):
    leaf_points = points.reshape(LEAVES, PTS_DEV, F)
    leaf_weights = weights.reshape(LEAVES, PTS_DEV, R)
    nothing = jnp.zeros((PTS_DEV, R), jnp.float32)

    def leaf_near(index):
        own = leaf_points[index]
        total = apply_tile(own, own, leaf_weights[index])
        for offset in range(1, REACH + 1):
            for column, other in ((offset - 1, index + offset), (REACH + offset - 1, index - offset)):
                listed = near_mask[index, column] > 0
                clipped = jnp.clip(other, 0, LEAVES - 1).astype(jnp.int32)
                total = total + lax.cond(listed, lambda c: apply_tile(own, leaf_points[c], leaf_weights[c]), lambda c: nothing, clipped)
        return total

    near_field = lax.map(leaf_near, jnp.arange(LEAVES, dtype=jnp.int32))

    def leaf_charges(args):
        own, own_w, pick = args
        skel_points = jnp.take(own, pick, axis=0)
        charges = jnp.dot(kernel(skel_points, own).astype(jnp.bfloat16), own_w, preferred_element_type=jnp.float32).astype(jnp.bfloat16)
        return skel_points, charges

    skel_points, charges = lax.map(leaf_charges, (leaf_points, leaf_weights, leaf_skeleton))
    far_field = jnp.zeros((LEAVES, PTS_DEV, R), jnp.float32)
    leaf_ids = jnp.arange(LEAVES, dtype=jnp.int32)
    for tree_level in range(LEVELS):
        partner = jnp.bitwise_xor(leaf_ids, 1 << tree_level)
        partner_points = skel_points[partner]
        partner_charges = charges[partner]

        def far_terms(args):
            own, remote_points, remote_charges = args
            return jnp.dot(kernel(own, remote_points).astype(jnp.bfloat16), remote_charges, preferred_element_type=jnp.float32)

        far_field = far_field + lax.map(far_terms, (leaf_points, partner_points, partner_charges))
        if tree_level + 1 < LEVELS:
            is_upper = (jnp.right_shift(leaf_ids, tree_level) & 1) == 1
            upper_mask = is_upper[:, None, None]
            union_points = jnp.concatenate([jnp.where(upper_mask, partner_points, skel_points), jnp.where(upper_mask, skel_points, partner_points)], axis=1)
            union_charges = jnp.concatenate([jnp.where(upper_mask, partner_charges, charges), jnp.where(upper_mask, charges, partner_charges)], axis=1)

            def climb(args):
                union_p, union_c, chosen = args
                node_points = jnp.take(union_p, chosen, axis=0)
                affinity = kernel(node_points, union_p)
                transfer_share = (affinity / jnp.sum(affinity, axis=0, keepdims=True)).astype(jnp.bfloat16)
                node_charges = jnp.dot(transfer_share, union_c, preferred_element_type=jnp.float32).astype(jnp.bfloat16)
                return node_points, node_charges

            skel_points, charges = lax.map(climb, (union_points, union_charges, node_skeleton[tree_level]))
    near_flat = near_field.reshape(NPTS, R)
    far_flat = far_field.reshape(NPTS, R)
    residual = targets.astype(jnp.float32) - ridge_weight * weights.astype(jnp.float32) - near_flat - far_flat
    updated = (weights.astype(jnp.float32) + damping * residual / (1.0 + ridge_weight)).astype(jnp.bfloat16)
    return updated, residual
```

```python
import functools

import jax
import jax.numpy as jnp
from jax import lax
from jax.experimental import pallas as pl
from jax.experimental.pallas import tpu as pltpu
from jax.sharding import PartitionSpec as P

LEVELS = 5

ridge_weight = 1.0
damping = 0.25
LOG2E = 1.4426950408889634

CHUNK = 256
BLOCK = 256


def pieces(rows):
    wide = rows.astype(jnp.float32)
    sq = jnp.sum(wide * wide, axis=1, keepdims=True)
    hi = sq.astype(jnp.bfloat16).astype(jnp.float32)
    rest = sq - hi
    mid = rest.astype(jnp.bfloat16).astype(jnp.float32)
    return hi, mid, rest - mid


def extra(rows, parts, first, second):
    hi, mid, low = parts
    lane = lax.broadcasted_iota(jnp.int32, rows.shape, 1)

    def picked(which, start):
        if which is None:
            return jnp.where((lane >= start) & (lane < start + 3), 1.0, 0.0)
        zero = jnp.zeros(rows.shape, jnp.float32)
        out = jnp.where(lane == start, hi, zero)
        out = jnp.where(lane == start + 1, mid, out)
        return jnp.where(lane == start + 2, low, out)

    return picked(first, 0) + picked(second, 3)


def left_form(rows, parts):
    tail = -extra(rows, parts, "norms", None)
    return jnp.concatenate(
        [(rows.astype(jnp.float32) * 2.0).astype(jnp.bfloat16), tail.astype(jnp.bfloat16)], axis=1
    )


def right_form(rows, parts):
    tail = extra(rows, parts, None, "norms")
    return jnp.concatenate([rows, tail.astype(jnp.bfloat16)], axis=1)


def affinity(left, right, features):
    s = lax.dot_general(left, right, (((1,), (1,)), ((), ())), preferred_element_type=jnp.float32)
    return jnp.exp2(s * (LOG2E / features))


def dot(a, b):
    return jnp.dot(a, b, preferred_element_type=jnp.float32)


def step(
    n,
    mask_ref,
    points_ref,
    weights_ref,
    targets_ref,
    index_ref,
    updated_ref,
    residual_ref,
    near_x,
    near_w,
    sib_x,
    sib_w,
    q_x,
    q_w,
    union,
    own_left,
    own_right,
    other_right,
    total,
    x_send,
    x_recv,
    r_send,
    r_recv,
    s_send,
    s_recv,
    q_send,
    q_recv,
    l_send,
    l_recv,
):
    me = lax.axis_index("leaf")
    rows, features = points_ref.shape
    skel = index_ref.shape[0]
    chunks = rows // CHUNK
    per_half = chunks // 2
    half = rows // 2
    core = lax.rem(me, 2)
    side = lax.rem(me // 2, 2)
    flip = core + side - 2 * core * side
    relay_to = me + 4 - 8 * side
    relay_from = me - 4 + 8 * side
    gives = (relay_to >= 0) & (relay_to < n)
    takes = (relay_from >= 0) & (relay_from < n)

    def bit(level):
        return lax.rem(me // (2**level), 2)

    def across(level):
        return me + (1 - 2 * bit(level)) * (2**level)

    barrier = pltpu.get_barrier_semaphore()
    for level in range(LEVELS):
        pl.semaphore_signal(barrier, inc=1, device_id=(across(level),), device_id_type=pl.DeviceIdType.MESH)

    @pl.when(gives)
    def _():
        pl.semaphore_signal(barrier, inc=1, device_id=(relay_to,), device_id_type=pl.DeviceIdType.MESH)

    @pl.when(takes)
    def _():
        pl.semaphore_signal(barrier, inc=1, device_id=(relay_from,), device_id_type=pl.DeviceIdType.MESH)

    pl.semaphore_wait(barrier, LEVELS + gives.astype(jnp.int32) + takes.astype(jnp.int32))

    def remote(src, dst, send, recv, device):
        return pltpu.make_async_remote_copy(
            src_ref=src, dst_ref=dst, send_sem=send, recv_sem=recv,
            device_id=(device,), device_id_type=pl.DeviceIdType.MESH,
        )

    def x_copies(k):
        part = pl.ds(k * CHUNK, CHUNK)
        return [
            remote(points_ref.at[part], near_x.at[0, part], x_send.at[k, 0], x_recv.at[k, 0], across(1)),
            remote(weights_ref.at[part], near_w.at[0, part], x_send.at[k, 1], x_recv.at[k, 1], across(1)),
        ]

    def r_copies(k):
        part = pl.ds(k * CHUNK, CHUNK)
        return [
            remote(near_x.at[0, part], near_x.at[1, part], r_send.at[k, 0], r_recv.at[k, 0], relay_to),
            remote(near_w.at[0, part], near_w.at[1, part], r_send.at[k, 1], r_recv.at[k, 1], relay_to),
        ]

    def q_copies(h, slot):
        part = pl.ds(h * half, half)
        return [
            remote(near_x.at[slot, part], q_x.at[part], q_send.at[h, 0], q_recv.at[h, 0], across(0)),
            remote(near_w.at[slot, part], q_w.at[part], q_send.at[h, 1], q_recv.at[h, 1], across(0)),
        ]

    def s_copies():
        return [
            remote(points_ref, sib_x, s_send.at[0], s_recv.at[0], across(0)),
            remote(weights_ref, sib_w, s_send.at[1], s_recv.at[1], across(0)),
        ]

    def l_copy(level):
        mine = union.at[level, bit(level)]
        return remote(mine, mine, l_send.at[level], l_recv.at[level], across(level))

    def start(copies):
        for copy in copies:
            copy.start()

    def landed(copies):
        for copy in copies:
            copy.wait_recv()

    def left_behind(copies):
        for copy in copies:
            copy.wait_send()

    def x_landed(k):
        landed(x_copies(k))

        @pl.when(gives)
        def _():
            start(r_copies(k))

    def near_unit(x_ref, w_ref, h, scale, own=False):
        part = slice(h * half, (h + 1) * half)
        if not own:
            x = x_ref[part, :]
            other_right[...] = right_form(x, pieces(x))

        def body(r, _):
            at = pl.ds(pl.multiple_of(r * BLOCK, BLOCK), BLOCK)
            right = own_right[part, :] if own else other_right[...]
            tile = affinity(own_left[at, :], right, features).astype(jnp.bfloat16)
            value = dot(tile, w_ref[part, :])
            if scale is not None:
                value = value * scale
            total[at, :] += value
            return 0

        lax.fori_loop(0, rows // BLOCK, body, 0)

    def far_unit(level):
        pair = union[level, 1 - bit(level)]
        p = pair[:, :features]
        other_right[:skel, :] = right_form(p, pieces(p))

        def body(r, _):
            at = pl.ds(pl.multiple_of(r * BLOCK, BLOCK), BLOCK)
            tile = affinity(own_left[at, :], other_right[:skel, :], features).astype(jnp.bfloat16)
            total[at, :] += dot(tile, union[level, 1 - bit(level), :, features:])
            return 0

        lax.fori_loop(0, rows // BLOCK, body, 0)

    def chosen(level, count):
        col = lax.broadcasted_iota(jnp.int32, (skel, count), 1)
        return jnp.where(col == index_ref[:, level : level + 1], 1.0, 0.0).astype(jnp.bfloat16)

    def climb(level):
        landed([l_copy(level)])
        low, high = union[level, 0], union[level, 1]
        p = jnp.concatenate([low[:, :features], high[:, :features]], axis=0)
        q = jnp.concatenate([low[:, features:], high[:, features:]], axis=0)
        sk = dot(chosen(level + 1, 2 * skel), p).astype(jnp.bfloat16)
        aff = affinity(left_form(sk, pieces(sk)), right_form(p, pieces(p)), features)
        share = (aff / jnp.sum(aff, axis=0, keepdims=True)).astype(jnp.bfloat16)
        union[level + 1, bit(level + 1), :, :features] = sk
        union[level + 1, bit(level + 1), :, features:] = dot(share, q).astype(jnp.bfloat16)
        l_copy(level + 1).start()

    def listed(column):
        return mask_ref[0, column].astype(jnp.float32)

    start(x_copies(0) + s_copies() + x_copies(1))

    x = points_ref[...]
    norms = pieces(x)
    own_right[...] = right_form(x, norms)
    sk = dot(chosen(0, rows), x).astype(jnp.bfloat16)
    tile = affinity(left_form(sk, pieces(sk)), own_right[...], features).astype(jnp.bfloat16)
    union[0, core, :, :features] = sk
    union[0, core, :, features:] = dot(tile, weights_ref[...]).astype(jnp.bfloat16)
    l_copy(0).start()
    own_left[...] = left_form(x, norms)
    total[...] = jnp.zeros_like(total)

    climb(0)
    for k in range(2, chunks):
        start(x_copies(k))
    near_unit(points_ref, weights_ref, 0, None, own=True)
    x_landed(0)
    far_unit(0)
    climb(1)
    near_unit(points_ref, weights_ref, 1, None, own=True)
    x_landed(1)
    far_unit(1)
    climb(2)
    landed(s_copies())
    near_unit(sib_x, sib_w, 0, listed(2 * core))
    far_unit(2)
    for k in range(2, per_half):
        x_landed(k)
    climb(3)
    near_unit(sib_x, sib_w, 1, listed(2 * core))
    far_unit(3)

    @pl.when(flip == 0)
    def _():
        start(q_copies(0, 0))

    near_unit(near_x.at[0], near_w.at[0], 0, listed(1 + 2 * side))
    x_landed(per_half)
    landed([l_copy(LEVELS - 1)])
    far_unit(LEVELS - 1)
    for k in range(per_half + 1, chunks - 1):
        x_landed(k)

    @pl.when(takes)
    def _():
        for k in range(per_half):
            landed(r_copies(k))

        @pl.when(flip == 1)
        def _():
            start(q_copies(0, 1))

        near_unit(near_x.at[1], near_w.at[1], 0, listed(3 - 2 * side))

    x_landed(chunks - 1)

    @pl.when(flip == 0)
    def _():
        start(q_copies(1, 0))

    near_unit(near_x.at[0], near_w.at[0], 1, listed(1 + 2 * side))

    takes_q = (flip == 1) | takes

    @pl.when(takes_q)
    def _():
        landed(q_copies(0, 0))
        near_unit(q_x, q_w, 0, listed(2 - 2 * core))

    @pl.when(takes)
    def _():
        for k in range(per_half, chunks):
            landed(r_copies(k))

        @pl.when(flip == 1)
        def _():
            start(q_copies(1, 1))

        near_unit(near_x.at[1], near_w.at[1], 1, listed(3 - 2 * side))

    @pl.when(takes_q)
    def _():
        landed(q_copies(1, 0))
        near_unit(q_x, q_w, 1, listed(2 - 2 * core))

    def finish(r, _):
        at = pl.ds(pl.multiple_of(r * BLOCK, BLOCK), BLOCK)
        w = weights_ref[at, :].astype(jnp.float32)
        res = targets_ref[at, :].astype(jnp.float32) - ridge_weight * w - total[at, :]
        residual_ref[at, :] = res
        updated_ref[at, :] = (w + damping * res / (1.0 + ridge_weight)).astype(jnp.bfloat16)
        return 0

    lax.fori_loop(0, rows // BLOCK, finish, 0)

    left_behind(s_copies())
    for k in range(chunks):
        left_behind(x_copies(k))
    for level in range(LEVELS):
        left_behind([l_copy(level)])

    @pl.when(gives)
    def _():
        for k in range(chunks):
            left_behind(r_copies(k))

    @pl.when((flip == 0) | takes)
    def _():
        for h in range(2):
            left_behind(q_copies(h, 0))


def local(n, points, weights, targets, near_mask, leaf_skeleton, node_skeleton):
    rows, features = points.shape
    rhs = weights.shape[1]
    skel = leaf_skeleton.shape[1]
    chunks = rows // CHUNK
    index = jnp.concatenate([leaf_skeleton, node_skeleton[:, 0]], axis=0).T
    vmem = pl.BlockSpec(memory_space=pltpu.VMEM)
    dma = pltpu.SemaphoreType.DMA
    bf16 = jnp.bfloat16
    return pl.pallas_call(
        functools.partial(step, n),
        out_shape=(
            jax.ShapeDtypeStruct((rows, rhs), bf16),
            jax.ShapeDtypeStruct((rows, rhs), jnp.float32),
        ),
        in_specs=[pl.BlockSpec(memory_space=pltpu.SMEM)] + [vmem] * 4,
        out_specs=(vmem, vmem),
        scratch_shapes=[
            pltpu.VMEM((2, rows, features), bf16),
            pltpu.VMEM((2, rows, rhs), bf16),
            pltpu.VMEM((rows, features), bf16),
            pltpu.VMEM((rows, rhs), bf16),
            pltpu.VMEM((rows, features), bf16),
            pltpu.VMEM((rows, rhs), bf16),
            pltpu.VMEM((LEVELS, 2, skel, features + rhs), bf16),
            pltpu.VMEM((rows, 2 * features), bf16),
            pltpu.VMEM((rows, 2 * features), bf16),
            pltpu.VMEM((rows // 2, 2 * features), bf16),
            pltpu.VMEM((rows, rhs), jnp.float32),
            dma((chunks, 2)),
            dma((chunks, 2)),
            dma((chunks, 2)),
            dma((chunks, 2)),
            dma((2,)),
            dma((2,)),
            dma((2, 2)),
            dma((2, 2)),
            dma((LEVELS,)),
            dma((LEVELS,)),
        ],
        compiler_params=pltpu.CompilerParams(
            collective_id=0, has_side_effects=True, vmem_limit_bytes=60 * 1024 * 1024
        ),
    )(near_mask, points, weights, targets, index)


def solution(mesh):
    placed = (
        P("leaf", None),
        P("leaf", None),
        P("leaf", None),
        P("leaf", None),
        P("leaf", None),
        P(None, "leaf", None),
    )
    return jax.shard_map(
        functools.partial(local, mesh.shape["leaf"]),
        mesh=mesh,
        in_specs=placed,
        out_specs=(P("leaf", None), P("leaf", None)),
        check_vma=False,
    )
```

```python
import functools

import jax
import jax.numpy as jnp
from jax import lax
from jax.experimental import pallas as pl
from jax.experimental.pallas import tpu as pltpu
from jax.sharding import PartitionSpec as P

LEVELS = 5

ridge_weight = 1.0
damping = 0.25
LOG2E = 1.4426950408889634

CHUNK = 256
BLOCK = 768


def pieces(rows):
    wide = rows.astype(jnp.float32)
    sq = jnp.sum(wide * wide, axis=1, keepdims=True)
    hi = sq.astype(jnp.bfloat16).astype(jnp.float32)
    rest = sq - hi
    mid = rest.astype(jnp.bfloat16).astype(jnp.float32)
    return hi, mid, rest - mid


def extra(rows, parts, first, second):
    hi, mid, low = parts
    lane = lax.broadcasted_iota(jnp.int32, rows.shape, 1)

    def picked(which, start):
        if which is None:
            return jnp.where((lane >= start) & (lane < start + 3), 1.0, 0.0)
        zero = jnp.zeros(rows.shape, jnp.float32)
        out = jnp.where(lane == start, hi, zero)
        out = jnp.where(lane == start + 1, mid, out)
        return jnp.where(lane == start + 2, low, out)

    return picked(first, 0) + picked(second, 3)


def left_form(rows, parts):
    tail = -extra(rows, parts, "norms", None)
    return jnp.concatenate(
        [(rows.astype(jnp.float32) * 2.0).astype(jnp.bfloat16), tail.astype(jnp.bfloat16)], axis=1
    )


def right_form(rows, parts):
    tail = extra(rows, parts, None, "norms")
    return jnp.concatenate([rows, tail.astype(jnp.bfloat16)], axis=1)


def affinity(left, right, features):
    s = lax.dot_general(left, right, (((1,), (1,)), ((), ())), preferred_element_type=jnp.float32)
    return jnp.exp2(s * (LOG2E / features))


def dot(a, b):
    return jnp.dot(a, b, preferred_element_type=jnp.float32)


def step(
    n,
    mask_ref,
    points_ref,
    weights_ref,
    leaf_index_ref,
    node_index_ref,
    total,
    near_x,
    near_w,
    sib_x,
    sib_w,
    q_x,
    q_w,
    union,
    own_left,
    own_right,
    other_right,
    other_w,
    indices,
    x_send,
    x_recv,
    r_send,
    r_recv,
    s_send,
    s_recv,
    q_send,
    q_recv,
    l_send,
    l_recv,
):
    me = lax.axis_index("leaf")
    rows, features = points_ref.shape
    skel = leaf_index_ref.shape[1]
    chunks = rows // CHUNK
    per_half = chunks // 2
    half = rows // 2
    core = lax.rem(me, 2)
    side = lax.rem(me // 2, 2)
    flip = core + side - 2 * core * side
    relay_to = me + 4 - 8 * side
    relay_from = me - 4 + 8 * side
    gives = (relay_to >= 0) & (relay_to < n)
    takes = (relay_from >= 0) & (relay_from < n)

    def bit(level):
        return lax.rem(me // (2**level), 2)

    def across(level):
        return me + (1 - 2 * bit(level)) * (2**level)

    barrier = pltpu.get_barrier_semaphore()
    for level in range(LEVELS):
        pl.semaphore_signal(barrier, inc=1, device_id=(across(level),), device_id_type=pl.DeviceIdType.MESH)

    @pl.when(gives)
    def _():
        pl.semaphore_signal(barrier, inc=1, device_id=(relay_to,), device_id_type=pl.DeviceIdType.MESH)

    @pl.when(takes)
    def _():
        pl.semaphore_signal(barrier, inc=1, device_id=(relay_from,), device_id_type=pl.DeviceIdType.MESH)

    pl.semaphore_wait(barrier, LEVELS + gives.astype(jnp.int32) + takes.astype(jnp.int32))

    def remote(src, dst, send, recv, device):
        return pltpu.make_async_remote_copy(
            src_ref=src, dst_ref=dst, send_sem=send, recv_sem=recv,
            device_id=(device,), device_id_type=pl.DeviceIdType.MESH,
        )

    def x_copies(k):
        part = pl.ds(k * CHUNK, CHUNK)
        return [
            remote(points_ref.at[part], near_x.at[0, part], x_send.at[k, 0], x_recv.at[k, 0], across(1)),
            remote(weights_ref.at[part], near_w.at[0, part], x_send.at[k, 1], x_recv.at[k, 1], across(1)),
        ]

    def r_copies(k):
        part = pl.ds(k * CHUNK, CHUNK)
        return [
            remote(near_x.at[0, part], near_x.at[1, part], r_send.at[k, 0], r_recv.at[k, 0], relay_to),
            remote(near_w.at[0, part], near_w.at[1, part], r_send.at[k, 1], r_recv.at[k, 1], relay_to),
        ]

    def q_copies(h, slot):
        part = pl.ds(h * half, half)
        return [
            remote(near_x.at[slot, part], q_x.at[part], q_send.at[h, 0], q_recv.at[h, 0], across(0)),
            remote(near_w.at[slot, part], q_w.at[part], q_send.at[h, 1], q_recv.at[h, 1], across(0)),
        ]

    def s_copies():
        return [
            remote(points_ref, sib_x, s_send.at[0], s_recv.at[0], across(0)),
            remote(weights_ref, sib_w, s_send.at[1], s_recv.at[1], across(0)),
        ]

    def l_copy(level):
        mine = union.at[level, bit(level)]
        return remote(mine, mine, l_send.at[level], l_recv.at[level], across(level))

    def start(copies):
        for copy in copies:
            copy.start()

    def landed(copies):
        for copy in copies:
            copy.wait_recv()

    def left_behind(copies):
        for copy in copies:
            copy.wait_send()

    def x_landed(k):
        landed(x_copies(k))

        @pl.when(gives)
        def _():
            start(r_copies(k))

    def near_unit(x_ref, w_ref, h, scale, own=False):
        part = slice(h * half, (h + 1) * half)
        if not own:
            x = x_ref[part, :]
            other_right[...] = right_form(x, pieces(x))

        def body(r, _):
            at = pl.ds(pl.multiple_of(r * BLOCK, BLOCK), BLOCK)
            right = own_right[part, :] if own else other_right[...]
            tile = affinity(own_left[at, :], right, features).astype(jnp.bfloat16)
            value = dot(tile, w_ref[part, :])
            if scale is not None:
                value = value * scale
            total[at, :] += value
            return 0

        lax.fori_loop(0, rows // BLOCK, body, 0)

    def far_unit(levels):
        depth = len(levels) * skel
        for i, level in enumerate(levels):
            part = slice(i * skel, (i + 1) * skel)
            pair = union[level, 1 - bit(level)]
            p = pair[:, :features]
            other_right[part, :] = right_form(p, pieces(p))
            other_w[part, :] = pair[:, features:]

        def body(r, _):
            at = pl.ds(pl.multiple_of(r * BLOCK, BLOCK), BLOCK)
            tile = affinity(own_left[at, :], other_right[:depth, :], features).astype(jnp.bfloat16)
            total[at, :] += dot(tile, other_w[:depth, :])
            return 0

        lax.fori_loop(0, rows // BLOCK, body, 0)

    def chosen(level, count):
        col = lax.broadcasted_iota(jnp.int32, (skel, count), 1).astype(jnp.float32)
        return jnp.where(col == indices[:, level : level + 1], 1.0, 0.0).astype(jnp.bfloat16)

    def climb(level):
        landed([l_copy(level)])
        low, high = union[level, 0], union[level, 1]
        p = jnp.concatenate([low[:, :features], high[:, :features]], axis=0)
        q = jnp.concatenate([low[:, features:], high[:, features:]], axis=0)
        sk = dot(chosen(level + 1, 2 * skel), p).astype(jnp.bfloat16)
        aff = affinity(left_form(sk, pieces(sk)), right_form(p, pieces(p)), features)
        share = (aff / jnp.sum(aff, axis=0, keepdims=True)).astype(jnp.bfloat16)
        union[level + 1, bit(level + 1), :, :features] = sk
        union[level + 1, bit(level + 1), :, features:] = dot(share, q).astype(jnp.bfloat16)
        l_copy(level + 1).start()

    def listed(column):
        return mask_ref[0, column].astype(jnp.float32)

    start(x_copies(0) + s_copies() + x_copies(1))

    table = [leaf_index_ref[...]] + [node_index_ref[level] for level in range(LEVELS - 1)]
    table = jnp.concatenate(table + [table[0]] * (8 - LEVELS), axis=0)
    indices[...] = table.astype(jnp.float32).T

    x = points_ref[...]
    norms = pieces(x)
    own_right[...] = right_form(x, norms)
    sk = dot(chosen(0, rows), x).astype(jnp.bfloat16)
    tile = affinity(left_form(sk, pieces(sk)), own_right[...], features).astype(jnp.bfloat16)
    union[0, core, :, :features] = sk
    union[0, core, :, features:] = dot(tile, weights_ref[...]).astype(jnp.bfloat16)
    l_copy(0).start()
    own_left[...] = left_form(x, norms)
    total[...] = jnp.zeros_like(total)

    climb(0)
    for k in range(2, chunks):
        start(x_copies(k))
    near_unit(points_ref, weights_ref, 0, None, own=True)
    x_landed(0)
    near_unit(points_ref, weights_ref, 1, None, own=True)
    climb(1)
    x_landed(1)
    landed(s_copies())
    near_unit(sib_x, sib_w, 0, listed(2 * core))
    climb(2)
    near_unit(sib_x, sib_w, 1, listed(2 * core))
    for k in range(2, per_half):
        x_landed(k)

    @pl.when(flip == 0)
    def _():
        start(q_copies(0, 0))

    climb(3)
    near_unit(near_x.at[0], near_w.at[0], 0, listed(1 + 2 * side))
    x_landed(per_half)
    far_unit([0, 1, 2])

    for k in range(per_half + 1, chunks - 1):
        x_landed(k)

    @pl.when(takes)
    def _():
        for k in range(per_half):
            landed(r_copies(k))

        @pl.when(flip == 1)
        def _():
            start(q_copies(0, 1))

        near_unit(near_x.at[1], near_w.at[1], 0, listed(3 - 2 * side))

    x_landed(chunks - 1)

    @pl.when(flip == 0)
    def _():
        start(q_copies(1, 0))

    near_unit(near_x.at[0], near_w.at[0], 1, listed(1 + 2 * side))

    takes_q = (flip == 1) | takes

    @pl.when(takes_q)
    def _():
        landed(q_copies(0, 0))
        near_unit(q_x, q_w, 0, listed(2 - 2 * core))

    landed([l_copy(LEVELS - 1)])
    far_unit([3, 4])

    @pl.when(takes)
    def _():
        for k in range(per_half, chunks):
            landed(r_copies(k))

        @pl.when(flip == 1)
        def _():
            start(q_copies(1, 1))

        near_unit(near_x.at[1], near_w.at[1], 1, listed(3 - 2 * side))

    @pl.when(takes_q)
    def _():
        landed(q_copies(1, 0))
        near_unit(q_x, q_w, 1, listed(2 - 2 * core))

    left_behind(s_copies())
    for k in range(chunks):
        left_behind(x_copies(k))
    for level in range(LEVELS):
        left_behind([l_copy(level)])

    @pl.when(gives)
    def _():
        for k in range(chunks):
            left_behind(r_copies(k))

    @pl.when((flip == 0) | takes)
    def _():
        for h in range(2):
            left_behind(q_copies(h, 0))


def local(n, points, weights, targets, near_mask, leaf_skeleton, node_skeleton):
    rows, features = points.shape
    rhs = weights.shape[1]
    skel = leaf_skeleton.shape[1]
    chunks = rows // CHUNK
    vmem = pl.BlockSpec(memory_space=pltpu.VMEM)
    dma = pltpu.SemaphoreType.DMA
    bf16 = jnp.bfloat16
    total = pl.pallas_call(
        functools.partial(step, n),
        out_shape=jax.ShapeDtypeStruct((rows, rhs), jnp.float32),
        in_specs=[pl.BlockSpec(memory_space=pltpu.SMEM)] + [vmem] * 4,
        out_specs=vmem,
        scratch_shapes=[
            pltpu.VMEM((2, rows, features), bf16),
            pltpu.VMEM((2, rows, rhs), bf16),
            pltpu.VMEM((rows, features), bf16),
            pltpu.VMEM((rows, rhs), bf16),
            pltpu.VMEM((rows, features), bf16),
            pltpu.VMEM((rows, rhs), bf16),
            pltpu.VMEM((LEVELS, 2, skel, features + rhs), bf16),
            pltpu.VMEM((rows, 2 * features), bf16),
            pltpu.VMEM((rows, 2 * features), bf16),
            pltpu.VMEM((rows // 2, 2 * features), bf16),
            pltpu.VMEM((rows // 2, rhs), bf16),
            pltpu.VMEM((skel, 8), jnp.float32),
            dma((chunks, 2)),
            dma((chunks, 2)),
            dma((chunks, 2)),
            dma((chunks, 2)),
            dma((2,)),
            dma((2,)),
            dma((2, 2)),
            dma((2, 2)),
            dma((LEVELS,)),
            dma((LEVELS,)),
        ],
        compiler_params=pltpu.CompilerParams(
            collective_id=0, has_side_effects=True, vmem_limit_bytes=60 * 1024 * 1024
        ),
    )(near_mask, points, weights, leaf_skeleton, node_skeleton)
    wide = weights.astype(jnp.float32)
    residual = targets.astype(jnp.float32) - ridge_weight * wide - total
    updated = (wide + damping * residual / (1.0 + ridge_weight)).astype(jnp.bfloat16)
    return updated, residual


def solution(mesh):
    placed = (
        P("leaf", None),
        P("leaf", None),
        P("leaf", None),
        P("leaf", None),
        P("leaf", None),
        P(None, "leaf", None),
    )
    return jax.shard_map(
        functools.partial(local, mesh.shape["leaf"]),
        mesh=mesh,
        in_specs=placed,
        out_specs=(P("leaf", None), P("leaf", None)),
        check_vma=False,
    )
```

```python
import functools

import jax
import jax.numpy as jnp
from jax import lax
from jax.experimental import pallas as pl
from jax.experimental.pallas import tpu as pltpu
from jax.sharding import PartitionSpec as P

LEVELS = 5

ridge_weight = 1.0
damping = 0.25
LOG2E = 1.4426950408889634

CHUNK = 256
BLOCK = 768


def pieces(rows):
    wide = rows.astype(jnp.float32)
    sq = jnp.sum(wide * wide, axis=1, keepdims=True)
    hi = sq.astype(jnp.bfloat16).astype(jnp.float32)
    rest = sq - hi
    mid = rest.astype(jnp.bfloat16).astype(jnp.float32)
    return hi, mid, rest - mid


def extra(rows, parts, first, second):
    hi, mid, low = parts
    lane = lax.broadcasted_iota(jnp.int32, rows.shape, 1)

    def picked(which, start):
        if which is None:
            return jnp.where((lane >= start) & (lane < start + 3), 1.0, 0.0)
        zero = jnp.zeros(rows.shape, jnp.float32)
        out = jnp.where(lane == start, hi, zero)
        out = jnp.where(lane == start + 1, mid, out)
        return jnp.where(lane == start + 2, low, out)

    return picked(first, 0) + picked(second, 3)


def left_form(rows, parts):
    tail = -extra(rows, parts, "norms", None)
    return jnp.concatenate(
        [(rows.astype(jnp.float32) * 2.0).astype(jnp.bfloat16), tail.astype(jnp.bfloat16)], axis=1
    )


def right_form(rows, parts):
    tail = extra(rows, parts, None, "norms")
    return jnp.concatenate([rows, tail.astype(jnp.bfloat16)], axis=1)


def affinity(left, right, features):
    s = lax.dot_general(left, right, (((1,), (1,)), ((), ())), preferred_element_type=jnp.float32)
    return jnp.exp2(s * (LOG2E / features))


def dot(a, b):
    return jnp.dot(a, b, preferred_element_type=jnp.float32)


def step(
    n,
    mask_ref,
    points_ref,
    weights_ref,
    leaf_index_ref,
    node_index_ref,
    total,
    near_x,
    near_w,
    sib_x,
    sib_w,
    q_x,
    q_w,
    union,
    own_left,
    own_right,
    other_right,
    other_w,
    indices,
    x_send,
    x_recv,
    r_send,
    r_recv,
    s_send,
    s_recv,
    q_send,
    q_recv,
    l_send,
    l_recv,
):
    me = lax.axis_index("leaf")
    rows, features = points_ref.shape
    skel = leaf_index_ref.shape[1]
    chunks = rows // CHUNK
    per_half = chunks // 2
    half = rows // 2
    core = lax.rem(me, 2)
    side = lax.rem(me // 2, 2)
    flip = core + side - 2 * core * side
    relay_to = me + 4 - 8 * side
    relay_from = me - 4 + 8 * side
    gives = (relay_to >= 0) & (relay_to < n)
    takes = (relay_from >= 0) & (relay_from < n)

    def bit(level):
        return lax.rem(me // (2**level), 2)

    def across(level):
        return me + (1 - 2 * bit(level)) * (2**level)

    barrier = pltpu.get_barrier_semaphore()
    for level in range(LEVELS):
        pl.semaphore_signal(barrier, inc=1, device_id=(across(level),), device_id_type=pl.DeviceIdType.MESH)

    @pl.when(gives)
    def _():
        pl.semaphore_signal(barrier, inc=1, device_id=(relay_to,), device_id_type=pl.DeviceIdType.MESH)

    @pl.when(takes)
    def _():
        pl.semaphore_signal(barrier, inc=1, device_id=(relay_from,), device_id_type=pl.DeviceIdType.MESH)

    pl.semaphore_wait(barrier, LEVELS + gives.astype(jnp.int32) + takes.astype(jnp.int32))

    def remote(src, dst, send, recv, device):
        return pltpu.make_async_remote_copy(
            src_ref=src, dst_ref=dst, send_sem=send, recv_sem=recv,
            device_id=(device,), device_id_type=pl.DeviceIdType.MESH,
        )

    def x_copies(k):
        part = pl.ds(k * CHUNK, CHUNK)
        return [
            remote(points_ref.at[part], near_x.at[0, part], x_send.at[k, 0], x_recv.at[k, 0], across(1)),
            remote(weights_ref.at[part], near_w.at[0, part], x_send.at[k, 1], x_recv.at[k, 1], across(1)),
        ]

    def r_copies(k):
        part = pl.ds(k * CHUNK, CHUNK)
        return [
            remote(near_x.at[0, part], near_x.at[1, part], r_send.at[k, 0], r_recv.at[k, 0], relay_to),
            remote(near_w.at[0, part], near_w.at[1, part], r_send.at[k, 1], r_recv.at[k, 1], relay_to),
        ]

    def q_copies(h, slot):
        part = pl.ds(h * half, half)
        return [
            remote(near_x.at[slot, part], q_x.at[part], q_send.at[h, 0], q_recv.at[h, 0], across(0)),
            remote(near_w.at[slot, part], q_w.at[part], q_send.at[h, 1], q_recv.at[h, 1], across(0)),
        ]

    def s_copies():
        return [
            remote(points_ref, sib_x, s_send.at[0], s_recv.at[0], across(0)),
            remote(weights_ref, sib_w, s_send.at[1], s_recv.at[1], across(0)),
        ]

    def l_copy(level):
        mine = union.at[level, bit(level)]
        return remote(mine, mine, l_send.at[level], l_recv.at[level], across(level))

    def start(copies):
        for copy in copies:
            copy.start()

    def landed(copies):
        for copy in copies:
            copy.wait_recv()

    def left_behind(copies):
        for copy in copies:
            copy.wait_send()

    def x_landed(k):
        landed(x_copies(k))

        @pl.when(gives)
        def _():
            start(r_copies(k))

    def near_unit(x_ref, w_ref, h, scale, own=False):
        part = slice(h * half, (h + 1) * half)
        if not own:
            x = x_ref[part, :]
            other_right[...] = right_form(x, pieces(x))

        def body(r, _):
            at = pl.ds(pl.multiple_of(r * BLOCK, BLOCK), BLOCK)
            right = own_right[part, :] if own else other_right[...]
            tile = affinity(own_left[at, :], right, features).astype(jnp.bfloat16)
            value = dot(tile, w_ref[part, :])
            if scale is not None:
                value = value * scale
            total[at, :] += value
            return 0

        lax.fori_loop(0, rows // BLOCK, body, 0)

    def far_unit(levels):
        depth = len(levels) * skel
        for i, level in enumerate(levels):
            part = slice(i * skel, (i + 1) * skel)
            pair = union[level, 1 - bit(level)]
            p = pair[:, :features]
            other_right[part, :] = right_form(p, pieces(p))
            other_w[part, :] = pair[:, features:]

        def body(r, _):
            at = pl.ds(pl.multiple_of(r * BLOCK, BLOCK), BLOCK)
            tile = affinity(own_left[at, :], other_right[:depth, :], features).astype(jnp.bfloat16)
            total[at, :] += dot(tile, other_w[:depth, :])
            return 0

        lax.fori_loop(0, rows // BLOCK, body, 0)

    def chosen(level, count):
        col = lax.broadcasted_iota(jnp.int32, (skel, count), 1).astype(jnp.float32)
        return jnp.where(col == indices[:, level : level + 1], 1.0, 0.0).astype(jnp.bfloat16)

    def climb(level):
        landed([l_copy(level)])
        low, high = union[level, 0], union[level, 1]
        p = jnp.concatenate([low[:, :features], high[:, :features]], axis=0)
        q = jnp.concatenate([low[:, features:], high[:, features:]], axis=0)
        sk = dot(chosen(level + 1, 2 * skel), p).astype(jnp.bfloat16)
        aff = affinity(left_form(sk, pieces(sk)), right_form(p, pieces(p)), features)
        share = (aff / jnp.sum(aff, axis=0, keepdims=True)).astype(jnp.bfloat16)
        union[level + 1, bit(level + 1), :, :features] = sk
        union[level + 1, bit(level + 1), :, features:] = dot(share, q).astype(jnp.bfloat16)
        l_copy(level + 1).start()

    def listed(column):
        return mask_ref[0, column].astype(jnp.float32)

    start(x_copies(0) + s_copies() + x_copies(1))

    table = [leaf_index_ref[...]] + [node_index_ref[level] for level in range(LEVELS - 1)]
    table = jnp.concatenate(table + [table[0]] * (8 - LEVELS), axis=0)
    indices[...] = table.astype(jnp.float32).T

    x = points_ref[...]
    norms = pieces(x)
    own_right[...] = right_form(x, norms)
    sk = dot(chosen(0, rows), x).astype(jnp.bfloat16)
    tile = affinity(left_form(sk, pieces(sk)), own_right[...], features).astype(jnp.bfloat16)
    union[0, core, :, :features] = sk
    union[0, core, :, features:] = dot(tile, weights_ref[...]).astype(jnp.bfloat16)
    l_copy(0).start()
    own_left[...] = left_form(x, norms)
    total[...] = jnp.zeros_like(total)

    climb(0)
    for k in range(2, chunks):
        start(x_copies(k))
    near_unit(points_ref, weights_ref, 0, None, own=True)
    for k in range(0, 1):
        x_landed(k)
    near_unit(points_ref, weights_ref, 1, None, own=True)
    for k in range(1, chunks // 3):
        x_landed(k)
    climb(1)
    landed(s_copies())
    near_unit(sib_x, sib_w, 0, listed(2 * core))
    for k in range(chunks // 3, per_half):
        x_landed(k)
    @pl.when(flip == 0)
    def _():
        start(q_copies(0, 0))

    climb(2)
    near_unit(sib_x, sib_w, 1, listed(2 * core))
    for k in range(per_half, chunks * 2 // 3):
        x_landed(k)
    near_unit(near_x.at[0], near_w.at[0], 0, listed(1 + 2 * side))
    climb(3)
    for k in range(chunks * 2 // 3, chunks - 1):
        x_landed(k)
    far_unit([0, 1, 2])
    for k in range(chunks - 1, chunks):
        x_landed(k)
    @pl.when(flip == 0)
    def _():
        start(q_copies(1, 0))


    @pl.when(takes)
    def _():
        for k in range(per_half):
            landed(r_copies(k))

        @pl.when(flip == 1)
        def _():
            start(q_copies(0, 1))

        near_unit(near_x.at[1], near_w.at[1], 0, listed(3 - 2 * side))

    near_unit(near_x.at[0], near_w.at[0], 1, listed(1 + 2 * side))

    takes_q = (flip == 1) | takes

    @pl.when(takes_q)
    def _():
        landed(q_copies(0, 0))
        near_unit(q_x, q_w, 0, listed(2 - 2 * core))

    landed([l_copy(LEVELS - 1)])
    far_unit([3, 4])

    @pl.when(takes)
    def _():
        for k in range(per_half, chunks):
            landed(r_copies(k))

        @pl.when(flip == 1)
        def _():
            start(q_copies(1, 1))

        near_unit(near_x.at[1], near_w.at[1], 1, listed(3 - 2 * side))

    @pl.when(takes_q)
    def _():
        landed(q_copies(1, 0))
        near_unit(q_x, q_w, 1, listed(2 - 2 * core))

    left_behind(s_copies())
    for k in range(chunks):
        left_behind(x_copies(k))
    for level in range(LEVELS):
        left_behind([l_copy(level)])

    @pl.when(gives)
    def _():
        for k in range(chunks):
            left_behind(r_copies(k))

    @pl.when((flip == 0) | takes)
    def _():
        for h in range(2):
            left_behind(q_copies(h, 0))


def local(n, points, weights, targets, near_mask, leaf_skeleton, node_skeleton):
    rows, features = points.shape
    rhs = weights.shape[1]
    skel = leaf_skeleton.shape[1]
    chunks = rows // CHUNK
    vmem = pl.BlockSpec(memory_space=pltpu.VMEM)
    dma = pltpu.SemaphoreType.DMA
    bf16 = jnp.bfloat16
    total = pl.pallas_call(
        functools.partial(step, n),
        out_shape=jax.ShapeDtypeStruct((rows, rhs), jnp.float32),
        in_specs=[pl.BlockSpec(memory_space=pltpu.SMEM)] + [vmem] * 4,
        out_specs=vmem,
        scratch_shapes=[
            pltpu.VMEM((2, rows, features), bf16),
            pltpu.VMEM((2, rows, rhs), bf16),
            pltpu.VMEM((rows, features), bf16),
            pltpu.VMEM((rows, rhs), bf16),
            pltpu.VMEM((rows, features), bf16),
            pltpu.VMEM((rows, rhs), bf16),
            pltpu.VMEM((LEVELS, 2, skel, features + rhs), bf16),
            pltpu.VMEM((rows, 2 * features), bf16),
            pltpu.VMEM((rows, 2 * features), bf16),
            pltpu.VMEM((rows // 2, 2 * features), bf16),
            pltpu.VMEM((rows // 2, rhs), bf16),
            pltpu.VMEM((skel, 8), jnp.float32),
            dma((chunks, 2)),
            dma((chunks, 2)),
            dma((chunks, 2)),
            dma((chunks, 2)),
            dma((2,)),
            dma((2,)),
            dma((2, 2)),
            dma((2, 2)),
            dma((LEVELS,)),
            dma((LEVELS,)),
        ],
        compiler_params=pltpu.CompilerParams(
            collective_id=0, has_side_effects=True, vmem_limit_bytes=60 * 1024 * 1024
        ),
    )(near_mask, points, weights, leaf_skeleton, node_skeleton)
    wide = weights.astype(jnp.float32)
    residual = targets.astype(jnp.float32) - ridge_weight * wide - total
    updated = (wide + damping * residual / (1.0 + ridge_weight)).astype(jnp.bfloat16)
    return updated, residual


def solution(mesh):
    placed = (
        P("leaf", None),
        P("leaf", None),
        P("leaf", None),
        P("leaf", None),
        P("leaf", None),
        P(None, "leaf", None),
    )
    return jax.shard_map(
        functools.partial(local, mesh.shape["leaf"]),
        mesh=mesh,
        in_specs=placed,
        out_specs=(P("leaf", None), P("leaf", None)),
        check_vma=False,
    )
```
